32 devices in a mesh: occ: 8 (over z, x), vir: 4 (over y, core).
Axes of the slice: x: 2, y: 2, z: 4, core: 2. Of those that a mesh axis runs over, the one named last changes fastest.
Arguments:
- b_occ: bfloat16 [32, 768, 2304], P('occ', 'vir'), may hold values from -0.86328125 to 0.86328125
- b_outer: bfloat16 [2, 768, 2304], P(None, 'vir', 'occ'), may hold values from -0.86328125 to 0.86328125
- eps_occ: float32 [32], P('occ'), may hold values from -1.5 to -0.3
- eps_outer: float32 [2], replicated, may hold values from -1.5 to -0.3
- eps_vir: float32 [768], P('vir'), may hold values from 0.2 to 3
Outputs:
- gamma_occ: float32 [32, 768, 2304], P('occ', 'vir')
- gamma_outer: float32 [2, 768, 2304], P(None, 'vir', 'occ')
The draws below stay inside these ranges and needn't reach their ends.
All inputs are finite; a program needn't handle non-finite values.
Results may differ from the reference program's by a relative error of at most 0.0018.
Values may be sent and summed in bfloat16 or wider, within the bound.
A program may use at most 128 MiB of HBM per device.

```python
import jax
import jax.numpy as jnp
from jax import lax

V = 768
P_SIZE = 2304
NJ = 2
NI = 32


def spiked(array, own_key, source, target, parts, factor):
    def block_of(position):
        return (jnp.arange(array.shape[position]) // (array.shape[position] // parts)).reshape((-1,) + (1,) * (array.ndim - 1 - position))

    one_side = jax.random.permutation(own_key, parts)[block_of(target)]
    other_side = (block_of(target) + parts // 2) % parts
    return jnp.where((block_of(source) == one_side) | (block_of(source) == other_side), factor * array, array)


def level_of(stream_key, shape, cuts, smallest, top_value):
    gain, own = 1.0, jax.random.fold_in(stream_key, 6)
    for position, blocks in cuts:
        steps = jnp.exp(jax.random.uniform(jax.random.fold_in(own, position), (blocks,), jnp.float32, smallest / len(cuts), top_value / len(cuts)))
        gain = gain * jnp.repeat(steps, shape[position] // blocks).reshape([-1 if axis == position else 1 for axis in range(len(shape))])
    return gain


def gaussian(key, extent, scale, bound, cuts=(), held_as=jnp.bfloat16):
    level = level_of(key, extent, cuts, -0.22, 0.18) if cuts else 1.0
    entries = jax.random.normal(key, extent, jnp.float32) * scale * level
    return jnp.minimum(jnp.maximum(entries, -bound), bound).astype(held_as)


def bell_draw_with(rng, shape, scale, reach, split, heavy, held_as=jnp.bfloat16):
    array = scale * jax.random.normal(rng, shape, jnp.float32)
    if split:
        array = array * level_of(rng, shape, split, -0.22, 0.18)
    return jnp.clip(spiked(array, jax.random.fold_in(rng, 3), *heavy), -reach, reach).astype(held_as)


def setup_inputs(seed: int = 0) -> dict:
    seeds = jax.random.split(jax.random.key(seed), 6)
    b_occ = bell_draw_with(seeds[0], (NI, V, P_SIZE), (P_SIZE ** -0.25), 0.86328125, ((0, 8), (1, 4)), (0, 2, 8, 2.0))
    b_outer = gaussian(seeds[1], (NJ, V, P_SIZE), (P_SIZE ** -0.25), 0.86328125, ((1, 4), (2, 8)))
    eps_occ = jnp.clip(-1.5 + 1.2 * jax.random.uniform(seeds[2], (NI,), jnp.float32) ** level_of(seeds[2], (NI,), ((0, 8),), -0.2, 0.2), -1.5, -0.3)
    eps_outer = jnp.clip(jax.random.uniform(seeds[3], (NJ,), jnp.float32, -1.5, -0.3), -1.5, -0.3)
    eps_vir = jnp.clip(0.2 + 2.8 * jax.random.uniform(seeds[4], (V,), jnp.float32) ** level_of(seeds[4], (V,), ((0, 4),), -0.2, 0.2), 0.2, 3.0)
    return dict(b_occ=b_occ, b_outer=b_outer, eps_occ=eps_occ, eps_outer=eps_outer, eps_vir=eps_vir)


def reference(b_occ, b_outer, eps_occ, eps_outer, eps_vir):
    flat = b_occ.reshape(NI * V, P_SIZE)
    flat_wide = flat.astype(jnp.float32)
    gamma_occ = jnp.zeros((NI * V, P_SIZE), jnp.float32)
    results = []
    for jpos in range(NJ):
        integral = jnp.dot(flat, b_outer[jpos].T, preferred_element_type=jnp.float32).reshape(NI, V, V)
        denom = eps_occ[:, None, None] + eps_outer[jpos] - eps_vir[None, :, None] - eps_vir[None, None, :]
        amps = integral / denom
        tilde = (2.0 * amps - jnp.swapaxes(amps, 1, 2)).reshape(NI * V, V)
        outer_wide = b_outer[jpos].astype(jnp.float32)
        gamma_occ = gamma_occ + jnp.dot(tilde, outer_wide, precision=lax.Precision.HIGHEST)
        results.append(jnp.dot(tilde.T, flat_wide, precision=lax.Precision.HIGHEST))
    return gamma_occ.reshape(NI, V, P_SIZE), jnp.stack(results)
```

```python
import functools

import jax
import jax.numpy as jnp
from jax import lax
from jax.experimental import pallas as pl
from jax.experimental.pallas import tpu as pltpu
from jax.sharding import PartitionSpec as P

MESH = pl.DeviceIdType.MESH
F32 = jnp.float32
BF16 = jnp.bfloat16
VMEM_SPEC = pl.BlockSpec(memory_space=pltpu.VMEM)
ANY_SPEC = pl.BlockSpec(memory_space=pl.ANY)
LIMIT = 60 * 1024 * 1024


def encode(x):
    square = x * x
    fourth = square * square
    return jnp.where(x < 0, -fourth, fourth).astype(BF16)


def decode(code):
    y = code.astype(F32)
    root = jnp.sqrt(jnp.sqrt(jnp.abs(y)))
    return jnp.where(y < 0, -root, root)


class Place:
    def __init__(self, n_g, n_u):
        o, v = lax.axis_index("occ"), lax.axis_index("vir")
        self.n_g, self.n_u = n_g, n_u
        self.o, self.v = o, v
        self.g, self.r = o // 2, o % 2
        self.u, self.c = v // 2, v % 2

    def up_g(self, s):
        return (self.g + s) % self.n_g

    def down_g(self, s):
        return (self.g + self.n_g - s) % self.n_g

    def up_u(self, t):
        return (self.u + t) % self.n_u

    def down_u(self, t):
        return (self.u + self.n_u - t) % self.n_u

    def x_peer(self):
        return (self.g * 2 + 1 - self.r, self.v)

    def c_peer(self):
        return (self.o, self.u * 2 + 1 - self.c)

    def y_peer(self, t):
        return (self.o, self.up_u(t) * 2 + self.c)

    def z_peer(self, s):
        return (self.up_g(s) * 2 + self.r, self.v)

    def greet(self, peers):
        barrier = pltpu.get_barrier_semaphore()
        for peer in peers:
            pl.semaphore_signal(barrier, inc=1, device_id=peer, device_id_type=MESH)
        pl.semaphore_wait(barrier, len(peers))


def remote(src, dst, send_sem, recv_sem, peer):
    return pltpu.make_async_remote_copy(
        src_ref=src, dst_ref=dst, send_sem=send_sem, recv_sem=recv_sem, device_id=peer, device_id_type=MESH
    )


def gather_kernel(n_g, n_u, own, eps, out, eps_out, local_sem, send, z_sem, x_sem, y_sem, d_sem, c_sem, e_send, e_sem):
    me = Place(n_g, n_u)
    n_vir = 2 * n_u
    vir_peers = [(me.o, (me.v + k) % n_vir) for k in range(1, n_vir)]
    me.greet([me.z_peer(s) for s in range(1, n_g)] + [me.x_peer()] + vir_peers)
    started = []

    def slot(g, r, u, c):
        return out.at[u * 2 + c, g * 2 + r]

    def go(src, place, recv_sem, peer):
        copy = remote(src, place, send.at[len(started)], recv_sem, peer)
        copy.start()
        started.append(copy)

    def arrived(place, sem):
        remote(place, place, send.at[0], sem, me.x_peer()).wait_recv()

    mine = slot(me.g, me.r, me.u, me.c)
    for s in range(1, n_g):
        go(own, mine, z_sem.at[s - 1], me.z_peer(s))
    go(own, mine, x_sem.at[0], me.x_peer())
    for t in range(1, n_u):
        go(own, mine, y_sem.at[0, t - 1], me.y_peer(t))
    go(own, mine, c_sem.at[0, 0, 0], me.c_peer())
    local = pltpu.make_async_copy(own, mine, local_sem.at[0])
    local.start()
    eps_local = pltpu.make_async_copy(eps, eps_out.at[me.v], local_sem.at[1])
    eps_local.start()
    eps_copies = [
        remote(eps, eps_out.at[me.v], e_send.at[k], e_sem.at[k], peer) for k, peer in enumerate(vir_peers)
    ]
    for copy in eps_copies:
        copy.start()

    def relay_z(s):
        place = slot(me.down_g(s), me.r, me.u, me.c)
        arrived(place, z_sem.at[s - 1])
        go(place, place, x_sem.at[s], me.x_peer())
        for t in range(1, n_u):
            go(place, place, y_sem.at[s, t - 1], me.y_peer(t))
        go(place, place, c_sem.at[s, 0, 0], me.c_peer())

    def relay_xy(s):
        place = slot(me.down_g(s), 1 - me.r, me.u, me.c)
        arrived(place, x_sem.at[s])
        if s % 2 == 0:
            for t in range(1, n_u):
                go(place, place, d_sem.at[s, t - 1], me.y_peer(t))
        go(place, place, c_sem.at[s, 1, 0], me.c_peer())
        for t in range(1, n_u):
            place = slot(me.down_g(s), me.r, me.down_u(t), me.c)
            arrived(place, y_sem.at[s, t - 1])
            if s % 2 == 1:
                go(place, place, d_sem.at[s, t - 1], me.x_peer())
            go(place, place, c_sem.at[s, 0, t], me.c_peer())

    for s in range(n_g):
        if s + 1 < n_g:
            relay_z(s + 1)
        relay_xy(s)
    for s in range(n_g):
        for t in range(1, n_u):
            place = slot(me.down_g(s), 1 - me.r, me.down_u(t), me.c)
            arrived(place, d_sem.at[s, t - 1])
            go(place, place, c_sem.at[s, 1, t], me.c_peer())
    for s in range(n_g):
        for q in range(2):
            for t in range(n_u):
                r = me.r if q == 0 else 1 - me.r
                arrived(slot(me.down_g(s), r, me.down_u(t), 1 - me.c), c_sem.at[s, q, t])
    local.wait()
    eps_local.wait()
    for k, copy in enumerate(eps_copies):
        copy.wait_send()
        source = (me.v + n_vir - 1 - k) % n_vir
        remote(eps, eps_out.at[source], e_send.at[k], e_sem.at[k], vir_peers[k]).wait_recv()
    for copy in started:
        copy.wait_send()


def gather(own, eps, n_g, n_u):
    qs, w = own.shape
    n_vir = 2 * n_u
    dma = pltpu.SemaphoreType.DMA
    messages = (n_g - 1) + n_g + 2 * n_g * (n_u - 1) + 2 * n_g * n_u
    return pl.pallas_call(
        functools.partial(gather_kernel, n_g, n_u),
        out_shape=(
            jax.ShapeDtypeStruct((n_vir, 2 * n_g, qs, w), own.dtype),
            jax.ShapeDtypeStruct((n_vir,) + eps.shape, eps.dtype),
        ),
        in_specs=[VMEM_SPEC, VMEM_SPEC],
        out_specs=(ANY_SPEC, VMEM_SPEC),
        scratch_shapes=[
            dma((2,)),
            dma((messages,)),
            dma((n_g,)),
            dma((n_g,)),
            dma((n_g, max(n_u - 1, 1))),
            dma((n_g, max(n_u - 1, 1))),
            dma((n_g, 2, n_u)),
            dma((n_vir - 1,)),
            dma((n_vir - 1,)),
        ],
        compiler_params=pltpu.CompilerParams(collective_id=0, has_side_effects=True, vmem_limit_bytes=LIMIT),
    )(own, eps)


def amplitude_kernel(
    n_vir, n_i, n_j, b_occ, b_whole, row, col, hi, lo, amps, sent, got, blocks, b_sem, send_sem, recv_sem
):
    o, v = lax.axis_index("occ"), lax.axis_index("vir")
    far = [(v + k) % n_vir for k in range(1, n_vir)]
    rows = b_occ.shape[0]
    vl = rows // n_i

    def load(k):
        source = (v + 1 + k) % n_vir
        return pltpu.make_async_copy(b_whole.at[source], blocks.at[k % 2], b_sem.at[k % 2])

    load(0).start()
    barrier = pltpu.get_barrier_semaphore()
    for peer in far:
        pl.semaphore_signal(barrier, inc=1, device_id=(o, peer), device_id_type=MESH)
    pl.semaphore_wait(barrier, n_vir - 1)

    copies = []
    for k in range(n_vir):
        target = (v + 1 + k) % n_vir
        if k + 1 < n_vir:
            load(k + 1).start()
        load(k).wait()

        def part(i, carry, k=k, target=target):
            at = pl.ds(pl.multiple_of(i * vl, vl), vl)
            integral = jnp.dot(b_occ[at, :], blocks[k % 2], preferred_element_type=F32)
            value = integral / (row[at, :] + col[target])
            amps[target, at, :] = value
            code = encode(value)
            if k + 1 < n_vir:
                sent[k, at, :] = code
            else:
                got[target, at, :] = code
            return carry

        lax.fori_loop(0, n_i, part, 0)
        if k + 1 < n_vir:
            copy = remote(sent.at[k], got.at[v], send_sem.at[k], recv_sem.at[k], (o, target))
            copy.start()
            copies.append(copy)

    def finish(source):
        def part(i, carry):
            at = pl.ds(pl.multiple_of(i * vl, vl), vl)
            turned = decode(got[source, at, :]).T
            swapped = jnp.concatenate([turned[j * vl : (j + 1) * vl] for j in range(n_j)], axis=1)
            tilde = 2.0 * amps[source, at, :] - swapped
            high = tilde.astype(BF16)
            hi[source, at, :] = high
            lo[source, at, :] = (tilde - high.astype(F32)).astype(BF16)
            return carry

        lax.fori_loop(0, n_i, part, 0)

    finish(v)
    for k in reversed(range(n_vir - 1)):
        source = (v + n_vir - 1 - k) % n_vir
        remote(sent.at[k], got.at[source], send_sem.at[k], recv_sem.at[k], (o, source)).wait_recv()
        finish(source)
    for copy in copies:
        copy.wait_send()


def amplitudes(b_occ, b_whole, row, col, n_i, n_j):
    n_vir, _, w = b_whole.shape
    rows = b_occ.shape[0]
    dma = pltpu.SemaphoreType.DMA
    shape = jax.ShapeDtypeStruct((n_vir, rows, w), BF16)
    return pl.pallas_call(
        functools.partial(amplitude_kernel, n_vir, n_i, n_j),
        out_shape=(shape, shape),
        in_specs=[VMEM_SPEC, ANY_SPEC, VMEM_SPEC, VMEM_SPEC],
        out_specs=(VMEM_SPEC, VMEM_SPEC),
        scratch_shapes=[
            pltpu.VMEM((n_vir, rows, w), F32),
            pltpu.VMEM((n_vir - 1, rows, w), BF16),
            pltpu.VMEM((n_vir, rows, w), BF16),
            pltpu.VMEM((2,) + b_whole.shape[1:], BF16),
            dma((2,)),
            dma((n_vir - 1,)),
            dma((n_vir - 1,)),
        ],
        compiler_params=pltpu.CompilerParams(collective_id=1, has_side_effects=True, vmem_limit_bytes=LIMIT),
    )(b_occ, b_whole, row, col)


def reduce_kernel(
    n_g, n_u, chunk, b_turned, b_whole, hi, lo, gamma, result,
    sums, c_out, c_in, out, d_in, x_in, y_in, z_in,
    c_send, c_sem, send, d_sem, x_sem, y_sem, z_sem,
):
    me = Place(n_g, n_u)
    n_vir = 2 * n_u
    qs = c_out.shape[2]
    depth = b_whole.shape[1]
    me.greet(
        [me.z_peer(s) for s in range(1, n_g)]
        + [me.x_peer(), me.c_peer()]
        + [me.y_peer(t) for t in range(1, n_u)]
    )
    started = []

    def product(s, q, c):
        g = (me.g + s) % n_g
        far, t = q // n_u, q % n_u
        r = (me.r + far) % 2
        v = (me.u + t) % n_u * 2 + c
        at = pl.ds(pl.multiple_of((g * 2 + r) * qs, qs), qs)
        left = b_turned[at, :]
        return jnp.dot(left, hi[v], preferred_element_type=F32) + jnp.dot(left, lo[v], preferred_element_type=F32)

    def go(src, dst, send_sem, recv_sem, peer):
        copy = remote(src, dst, send_sem, recv_sem, peer)
        copy.start()
        started.append(copy)

    def arrived(dst, sem):
        remote(dst, dst, sem, sem, me.x_peer()).wait_recv()

    def ship(s, q, dst, sem, peer):
        out[s, q] = encode(sums[s, q])
        go(out.at[s, q], dst, send.at[s, q], sem, peer)

    def take(s, q, src, sem):
        arrived(src, sem)
        sums[s, q] = sums[s, q] + decode(src[...])

    done = [0]

    def fill(count):
        def part(k, carry):
            at = pl.ds(pl.multiple_of(k * chunk, chunk), chunk)
            total = None
            for v in range(n_vir):
                right = b_whole[v, at, :]
                for left in (hi, lo):
                    term = lax.dot_general(
                        left[v], right, (((1,), (1,)), ((), ())), preferred_element_type=F32
                    )
                    total = term if total is None else total + term
            gamma[:, at] = total
            return carry

        last = min(done[0] + count, depth // chunk)
        if last > done[0]:
            lax.fori_loop(done[0], last, part, 0)
        done[0] = last

    share = max(depth // chunk // 6, 1)
    turn = [s % n_g for s in range(1, n_g + 1)]
    for s in turn:

        def theirs(q, carry, s=s):
            c_out[s, q] = encode(product(s, q, 1 - me.c))
            return carry

        lax.fori_loop(0, 2 * n_u, theirs, 0)
        for q in range(2 * n_u):
            go(c_out.at[s, q], c_in.at[s, q], c_send.at[s, q], c_sem.at[s, q], me.c_peer())

        def ours(q, carry, s=s):
            sums[s, q] = product(s, q, me.c)
            return carry

        lax.fori_loop(0, 2 * n_u, ours, 0)
        for q in range(2 * n_u):
            take(s, q, c_in.at[s, q], c_sem.at[s, q])
        for t in range(1, n_u):
            if s % 2 == 0:
                ship(s, n_u + t, d_in.at[s, t - 1], d_sem.at[s, t - 1], me.y_peer(t))
            else:
                ship(s, n_u + t, d_in.at[s, t - 1], d_sem.at[s, t - 1], me.x_peer())
        if s % 2 == 0:
            for t in range(1, n_u):
                ship(s, t, y_in.at[s, t - 1], y_sem.at[s, t - 1], me.y_peer(t))
        else:
            ship(s, n_u, x_in.at[s], x_sem.at[s], me.x_peer())
    fill(share)
    for s in turn:
        for t in range(1, n_u):
            q = n_u if s % 2 == 0 else t
            take(s, q, d_in.at[s, t - 1], d_sem.at[s, t - 1])
        if s % 2 == 0:
            ship(s, n_u, x_in.at[s], x_sem.at[s], me.x_peer())
        else:
            for t in range(1, n_u):
                ship(s, t, y_in.at[s, t - 1], y_sem.at[s, t - 1], me.y_peer(t))
        fill(share)
    for s in turn:
        take(s, 0, x_in.at[s], x_sem.at[s])
        for t in range(1, n_u):
            take(s, 0, y_in.at[s, t - 1], y_sem.at[s, t - 1])
        if s:
            ship(s, 0, z_in.at[s - 1], z_sem.at[s - 1], me.z_peer(s))
    fill(depth // chunk)
    for s in range(1, n_g):
        take(0, 0, z_in.at[s - 1], z_sem.at[s - 1])
    result[...] = sums[0, 0]
    for copy in started:
        copy.wait_send()


def reduce(b_turned, b_whole, hi, lo, n_g, n_u):
    depth, rows = b_turned.shape
    w = b_whole.shape[2]
    qs = depth // (2 * n_g)
    dma = pltpu.SemaphoreType.DMA
    chunk = max(k for k in range(128, 385, 128) if depth % k == 0)
    far = max(n_u - 1, 1)
    every = (n_g, 2 * n_u, qs, w)
    return pl.pallas_call(
        functools.partial(reduce_kernel, n_g, n_u, chunk),
        out_shape=(jax.ShapeDtypeStruct((rows, depth), F32), jax.ShapeDtypeStruct((qs, w), F32)),
        in_specs=[VMEM_SPEC] * 4,
        out_specs=(VMEM_SPEC, VMEM_SPEC),
        scratch_shapes=[
            pltpu.VMEM(every, F32),
            pltpu.VMEM(every, BF16),
            pltpu.VMEM(every, BF16),
            pltpu.VMEM(every, BF16),
            pltpu.VMEM((n_g, far, qs, w), BF16),
            pltpu.VMEM((n_g, qs, w), BF16),
            pltpu.VMEM((n_g, far, qs, w), BF16),
            pltpu.VMEM((n_g, qs, w), BF16),
            dma(every[:2]),
            dma(every[:2]),
            dma(every[:2]),
            dma((n_g, far)),
            dma((n_g,)),
            dma((n_g, far)),
            dma((n_g,)),
        ],
        compiler_params=pltpu.CompilerParams(collective_id=2, has_side_effects=True, vmem_limit_bytes=LIMIT),
    )(b_turned, b_whole, hi, lo)


def on_device(n_occ, n_vir, b_occ, b_outer, eps_occ, eps_outer, eps_vir):
    n_g, n_u = n_occ // 2, n_vir // 2
    n_i, vl, depth = b_occ.shape
    n_j, _, qs = b_outer.shape
    own = b_outer.transpose(2, 0, 1).reshape(qs, n_j * vl)
    eps_rows = jnp.broadcast_to(eps_vir[None, :], (8, vl))
    b_whole, eps_all = gather(own, eps_rows, n_g, n_u)
    b_whole = b_whole.reshape(n_vir, depth, n_j * vl)
    row = (eps_occ[:, None] - eps_vir[None, :]).reshape(n_i * vl, 1)
    col = (eps_outer[None, :, None] - eps_all[:, None, 0, :]).reshape(n_vir, 1, n_j * vl)
    flat = b_occ.reshape(n_i * vl, depth)
    hi, lo = amplitudes(flat, b_whole, row, col, n_i, n_j)
    gamma_occ, mine = reduce(flat.T, b_whole, hi, lo, n_g, n_u)
    gamma_outer = mine.reshape(qs, n_j, vl).transpose(1, 2, 0)
    return gamma_occ.reshape(b_occ.shape), gamma_outer


def solution(mesh):
    placed = (P("occ", "vir", None), P(None, "vir", "occ"), P("occ"), P(), P("vir"))
    return jax.shard_map(
        functools.partial(on_device, mesh.shape["occ"], mesh.shape["vir"]),
        mesh=mesh,
        in_specs=placed,
        out_specs=(P("occ", "vir", None), P(None, "vir", "occ")),
        check_vma=False,
    )
```

```python
import functools

import jax
import jax.numpy as jnp
from jax import lax
from jax.experimental import pallas as pl
from jax.experimental.pallas import tpu as pltpu
from jax.sharding import PartitionSpec as P

MESH = pl.DeviceIdType.MESH
F32 = jnp.float32
BF16 = jnp.bfloat16
VMEM_SPEC = pl.BlockSpec(memory_space=pltpu.VMEM)
SMEM_SPEC = pl.BlockSpec(memory_space=pltpu.SMEM)
ANY_SPEC = pl.BlockSpec(memory_space=pl.ANY)
LIMIT = 60 * 1024 * 1024


def encode(x):
    square = x * x
    fourth = square * square
    return jnp.where(x < 0, -fourth, fourth).astype(BF16)


def decode(code):
    y = code.astype(F32)
    root = lax.rsqrt(lax.rsqrt(jnp.abs(y)))
    return jnp.where(y < 0, -root, root)


class Place:
    def __init__(self, n_g, n_u):
        o, v = lax.axis_index("occ"), lax.axis_index("vir")
        self.n_g, self.n_u = n_g, n_u
        self.o, self.v = o, v
        self.g, self.r = o // 2, o % 2
        self.u, self.c = v // 2, v % 2

    def up_g(self, s):
        return (self.g + s) % self.n_g

    def down_g(self, s):
        return (self.g + self.n_g - s) % self.n_g

    def up_u(self, t):
        return (self.u + t) % self.n_u

    def down_u(self, t):
        return (self.u + self.n_u - t) % self.n_u

    def x_peer(self):
        return (self.g * 2 + 1 - self.r, self.v)

    def c_peer(self):
        return (self.o, self.u * 2 + 1 - self.c)

    def y_peer(self, t):
        return (self.o, self.up_u(t) * 2 + self.c)

    def z_peer(self, s):
        return (self.up_g(s) * 2 + self.r, self.v)

    def greet(self, peers):
        barrier = pltpu.get_barrier_semaphore()
        for peer in peers:
            pl.semaphore_signal(barrier, inc=1, device_id=peer, device_id_type=MESH)
        pl.semaphore_wait(barrier, len(peers))


def remote(src, dst, send_sem, recv_sem, peer):
    return pltpu.make_async_remote_copy(
        src_ref=src, dst_ref=dst, send_sem=send_sem, recv_sem=recv_sem, device_id=peer, device_id_type=MESH
    )


def gather_kernel(n_g, n_u, own, eps, b_occ, out, eps_out, b_turned, b_in, b_out, local_sem, send, z_sem, x_sem, y_sem, d_sem, c_sem, e_send, e_sem):
    me = Place(n_g, n_u)
    n_vir = 2 * n_u
    fetch = pltpu.make_async_copy(b_occ, b_in, local_sem.at[2])
    fetch.start()
    vir_peers = [(me.o, (me.v + k) % n_vir) for k in range(1, n_vir)]
    me.greet([me.z_peer(s) for s in range(1, n_g)] + [me.x_peer()] + vir_peers)
    started = []

    def slot(g, r, u, c):
        return out.at[u * 2 + c, g * 2 + r]

    def go(src, place, recv_sem, peer):
        copy = remote(src, place, send.at[len(started)], recv_sem, peer)
        copy.start()
        started.append(copy)

    def arrived(place, sem):
        remote(place, place, send.at[0], sem, me.x_peer()).wait_recv()

    mine = slot(me.g, me.r, me.u, me.c)
    for s in range(1, n_g):
        go(own, mine, z_sem.at[s - 1], me.z_peer(s))
    go(own, mine, x_sem.at[0], me.x_peer())
    for t in range(1, n_u):
        go(own, mine, y_sem.at[0, t - 1], me.y_peer(t))
    go(own, mine, c_sem.at[0, 0, 0], me.c_peer())
    local = pltpu.make_async_copy(own, mine, local_sem.at[0])
    local.start()
    eps_local = pltpu.make_async_copy(eps, eps_out.at[me.v], local_sem.at[1])
    eps_local.start()
    eps_copies = [
        remote(eps, eps_out.at[me.v], e_send.at[k], e_sem.at[k], peer) for k, peer in enumerate(vir_peers)
    ]
    for copy in eps_copies:
        copy.start()

    def relay_z(s):
        place = slot(me.down_g(s), me.r, me.u, me.c)
        arrived(place, z_sem.at[s - 1])
        go(place, place, x_sem.at[s], me.x_peer())
        for t in range(1, n_u):
            go(place, place, y_sem.at[s, t - 1], me.y_peer(t))
        go(place, place, c_sem.at[s, 0, 0], me.c_peer())

    def relay_xy(s):
        place = slot(me.down_g(s), 1 - me.r, me.u, me.c)
        arrived(place, x_sem.at[s])
        if s % 2 == 0:
            for t in range(1, n_u):
                go(place, place, d_sem.at[s, t - 1], me.y_peer(t))
        go(place, place, c_sem.at[s, 1, 0], me.c_peer())
        for t in range(1, n_u):
            place = slot(me.down_g(s), me.r, me.down_u(t), me.c)
            arrived(place, y_sem.at[s, t - 1])
            if s % 2 == 1:
                go(place, place, d_sem.at[s, t - 1], me.x_peer())
            go(place, place, c_sem.at[s, 0, t], me.c_peer())

    depth = b_in.shape[1]
    tile = next(k for k in (256, 128) if depth % k == 0)

    def turn(k, carry):
        at = pl.ds(pl.multiple_of(k * tile, tile), tile)
        b_out[at, :] = b_in[:, at].T
        return carry

    tiles = depth // tile
    edges = [tiles * k // n_g for k in range(n_g + 1)]
    for s in range(n_g):
        if s + 1 < n_g:
            relay_z(s + 1)
        if s == 0:
            fetch.wait()
        relay_xy(s)
        lax.fori_loop(edges[s], edges[s + 1], turn, 0)
    store = pltpu.make_async_copy(b_out, b_turned, local_sem.at[2])
    store.start()
    for s in range(n_g):
        for t in range(1, n_u):
            place = slot(me.down_g(s), 1 - me.r, me.down_u(t), me.c)
            arrived(place, d_sem.at[s, t - 1])
            go(place, place, c_sem.at[s, 1, t], me.c_peer())
    for s in range(n_g):
        for q in range(2):
            for t in range(n_u):
                r = me.r if q == 0 else 1 - me.r
                arrived(slot(me.down_g(s), r, me.down_u(t), 1 - me.c), c_sem.at[s, q, t])
    local.wait()
    eps_local.wait()
    store.wait()
    for k, copy in enumerate(eps_copies):
        copy.wait_send()
        source = (me.v + n_vir - 1 - k) % n_vir
        remote(eps, eps_out.at[source], e_send.at[k], e_sem.at[k], vir_peers[k]).wait_recv()
    for copy in started:
        copy.wait_send()


def gather(own, eps, b_occ, n_g, n_u):
    qs, w = own.shape
    n_vir = 2 * n_u
    dma = pltpu.SemaphoreType.DMA
    messages = (n_g - 1) + n_g + 2 * n_g * (n_u - 1) + 2 * n_g * n_u
    return pl.pallas_call(
        functools.partial(gather_kernel, n_g, n_u),
        out_shape=(
            jax.ShapeDtypeStruct((n_vir, 2 * n_g, qs, w), own.dtype),
            jax.ShapeDtypeStruct((n_vir,) + eps.shape, eps.dtype),
            jax.ShapeDtypeStruct(b_occ.shape[::-1], b_occ.dtype),
        ),
        in_specs=[VMEM_SPEC, VMEM_SPEC, ANY_SPEC],
        out_specs=(ANY_SPEC, VMEM_SPEC, ANY_SPEC),
        scratch_shapes=[
            pltpu.VMEM(b_occ.shape, b_occ.dtype),
            pltpu.VMEM(b_occ.shape[::-1], b_occ.dtype),
            dma((3,)),
            dma((messages,)),
            dma((n_g,)),
            dma((n_g,)),
            dma((n_g, max(n_u - 1, 1))),
            dma((n_g, max(n_u - 1, 1))),
            dma((n_g, 2, n_u)),
            dma((n_vir - 1,)),
            dma((n_vir - 1,)),
        ],
        compiler_params=pltpu.CompilerParams(collective_id=0, has_side_effects=True, vmem_limit_bytes=LIMIT),
    )(own, eps, b_occ)


def amplitude_kernel(
    n_vir, n_i, n_j, b_occ, b_whole, e_occ, e_outer, e_mine, e_all,
    hi, lo, amps, sent, got, blocks, b_sem, send_sem, recv_sem,
):
    o, v = lax.axis_index("occ"), lax.axis_index("vir")
    u, c, n_u = v // 2, v % 2, n_vir // 2
    steps = [(t, e) for t in range(1, n_u) for e in range(2)] + [(0, 1), (0, 0)]
    far = n_vir - 1
    targets = [(u + t) % n_u * 2 + (c + e) % 2 for t, e in steps]
    sources = [(u + n_u - t) % n_u * 2 + (c + e) % 2 for t, e in steps]
    rows = b_occ.shape[0]
    vl = rows // n_i

    def load(k):
        return pltpu.make_async_copy(b_whole.at[targets[k]], blocks.at[k % 2], b_sem.at[k % 2])

    load(0).start()
    barrier = pltpu.get_barrier_semaphore()
    for peer in targets[:far]:
        pl.semaphore_signal(barrier, inc=1, device_id=(o, peer), device_id_type=MESH)
    pl.semaphore_wait(barrier, far)

    row = e_mine[...].T[:, 0:1]
    copies = []
    for k, target in enumerate(targets):
        if k + 1 < n_vir:
            load(k + 1).start()
        load(k).wait()
        amps[target] = jnp.dot(b_occ[...], blocks[k % 2], preferred_element_type=F32)
        col = jnp.concatenate([e_outer[j] - e_all[target, 0:1, :] for j in range(n_j)], axis=1)

        def part(i, carry, k=k, target=target, col=col):
            at = pl.ds(pl.multiple_of(i * vl, vl), vl)
            value = amps[target, at, :] / ((e_occ[i] - row) + col)
            amps[target, at, :] = value
            code = encode(value)
            if k < far:
                sent[k, at, :] = code
            else:
                got[target, at, :] = code
            return carry

        lax.fori_loop(0, n_i, part, 0)
        if k < far:
            copy = remote(sent.at[k], got.at[v], send_sem.at[k], recv_sem.at[k], (o, target))
            copy.start()
            copies.append(copy)

    def finish(source):
        def part(i, carry):
            at = pl.ds(pl.multiple_of(i * vl, vl), vl)
            turned = decode(got[source, at, :]).T
            swapped = jnp.concatenate([turned[j * vl : (j + 1) * vl] for j in range(n_j)], axis=1)
            tilde = 2.0 * amps[source, at, :] - swapped
            high = tilde.astype(BF16)
            hi[source, at, :] = high
            lo[source, at, :] = (tilde - high.astype(F32)).astype(BF16)
            return carry

        lax.fori_loop(0, n_i, part, 0)

    finish(v)
    for k in [far - 1] + list(range(far - 1)):
        source = sources[k]
        remote(sent.at[k], got.at[source], send_sem.at[k], recv_sem.at[k], (o, source)).wait_recv()
        finish(source)
    for copy in copies:
        copy.wait_send()


def amplitudes(b_occ, b_whole, e_occ, e_outer, e_mine, e_all):
    n_i, n_j = e_occ.shape[0], e_outer.shape[0]
    n_vir, _, w = b_whole.shape
    rows = b_occ.shape[0]
    dma = pltpu.SemaphoreType.DMA
    shape = jax.ShapeDtypeStruct((n_vir, rows, w), BF16)
    return pl.pallas_call(
        functools.partial(amplitude_kernel, n_vir, n_i, n_j),
        out_shape=(shape, shape),
        in_specs=[VMEM_SPEC, ANY_SPEC, SMEM_SPEC, SMEM_SPEC, VMEM_SPEC, VMEM_SPEC],
        out_specs=(VMEM_SPEC, VMEM_SPEC),
        scratch_shapes=[
            pltpu.VMEM((n_vir, rows, w), F32),
            pltpu.VMEM((n_vir - 1, rows, w), BF16),
            pltpu.VMEM((n_vir, rows, w), BF16),
            pltpu.VMEM((2,) + b_whole.shape[1:], BF16),
            dma((2,)),
            dma((n_vir - 1,)),
            dma((n_vir - 1,)),
        ],
        compiler_params=pltpu.CompilerParams(collective_id=1, has_side_effects=True, vmem_limit_bytes=LIMIT),
    )(b_occ, b_whole, e_occ, e_outer, e_mine, e_all)


def reduce_kernel(
    n_g, n_u, chunk, b_turned, b_whole, hi, lo, gamma, result,
    b_local, held, sums, c_out, c_in, out, d_in, x_in, y_in, z_in,
    b_sem, g_sem, c_send, c_sem, send, d_sem, x_sem, y_sem, z_sem,
):
    me = Place(n_g, n_u)
    n_vir = 2 * n_u
    qs = c_out.shape[2]
    depth = b_whole.shape[1]
    fetch = pltpu.make_async_copy(b_whole, b_local, b_sem)
    fetch.start()
    me.greet(
        [me.z_peer(s) for s in range(1, n_g)]
        + [me.x_peer(), me.c_peer()]
        + [me.y_peer(t) for t in range(1, n_u)]
    )
    started = []

    def product(s, t, c, store):
        g = (me.g + s) % n_g
        v = (me.u + t) % n_u * 2 + c
        at = pl.ds(pl.multiple_of(g * 2 * qs, 2 * qs), 2 * qs)
        both = jnp.dot(
            b_turned[at, :], jnp.concatenate([hi[v], lo[v]], axis=1), preferred_element_type=F32
        )
        width = hi.shape[2]
        both = both[:, :width] + both[:, width:]
        store(me.r * n_u + t, both[:qs])
        store((1 - me.r) * n_u + t, both[qs:])

    def go(src, dst, send_sem, recv_sem, peer):
        copy = remote(src, dst, send_sem, recv_sem, peer)
        copy.start()
        started.append(copy)

    def arrived(dst, sem):
        remote(dst, dst, sem, sem, me.x_peer()).wait_recv()

    def ship(s, q, dst, sem, peer):
        out[s, q] = encode(sums[s, q])
        go(out.at[s, q], dst, send.at[s, q], sem, peer)

    def take(s, q, src, sem):
        arrived(src, sem)
        sums[s, q] = sums[s, q] + decode(src[...])

    done = [0]

    def out_copy(k):
        slot = k % 2
        at = pl.ds(pl.multiple_of(k * chunk, chunk), chunk)
        return pltpu.make_async_copy(held.at[slot], gamma.at[:, at], g_sem.at[slot])

    def fill(count):
        def part(k, carry):
            @pl.when(k >= 2)
            def _():
                out_copy(k - 2).wait()

            at = pl.ds(pl.multiple_of(k * chunk, chunk), chunk)
            right = jnp.concatenate([b_local[v, at, :] for v in range(n_vir)], axis=1)
            total = None
            for part_of in (hi, lo):
                left = jnp.concatenate([part_of[v] for v in range(n_vir)], axis=1)
                term = lax.dot_general(left, right, (((1,), (1,)), ((), ())), preferred_element_type=F32)
                total = term if total is None else total + term
            held[k % 2] = total
            out_copy(k).start()
            return carry

        if done[0] == 0:
            fetch.wait()
        last = min(done[0] + count, depth // chunk)
        if last > done[0]:
            lax.fori_loop(done[0], last, part, 0)
        done[0] = last

    share = max(depth // chunk // 4, 1)
    turn = [s % n_g for s in range(1, n_g + 1)]

    def first(s):
        def keep(q, value):
            sums[s, q] = value

        def code(q, value):
            c_out[s, q] = encode(value)

        def theirs(t, carry):
            product(s, t, 1 - me.c, code)
            return carry

        def ours(t, carry):
            product(s, t, me.c, keep)
            return carry

        lax.fori_loop(0, n_u, theirs, 0)
        for q in range(2 * n_u):
            go(c_out.at[s, q], c_in.at[s, q], c_send.at[s, q], c_sem.at[s, q], me.c_peer())
        lax.fori_loop(0, n_u, ours, 0)
        for q in reversed(range(2 * n_u)):
            take(s, q, c_in.at[s, q], c_sem.at[s, q])
            t = q - n_u
            if t > 0:
                peer = me.y_peer(t) if s % 2 == 0 else me.x_peer()
                ship(s, q, d_in.at[s, t - 1], d_sem.at[s, t - 1], peer)
        if s % 2 == 0:
            for t in range(1, n_u):
                ship(s, t, y_in.at[s, t - 1], y_sem.at[s, t - 1], me.y_peer(t))
        else:
            ship(s, n_u, x_in.at[s], x_sem.at[s], me.x_peer())

    def second(s):
        for t in range(1, n_u):
            q = n_u if s % 2 == 0 else t
            take(s, q, d_in.at[s, t - 1], d_sem.at[s, t - 1])
        if s % 2 == 0:
            ship(s, n_u, x_in.at[s], x_sem.at[s], me.x_peer())
        else:
            for t in range(1, n_u):
                ship(s, t, y_in.at[s, t - 1], y_sem.at[s, t - 1], me.y_peer(t))

    def third(s):
        take(s, 0, x_in.at[s], x_sem.at[s])
        for t in range(1, n_u):
            take(s, 0, y_in.at[s, t - 1], y_sem.at[s, t - 1])
        if s:
            ship(s, 0, z_in.at[s - 1], z_sem.at[s - 1], me.z_peer(s))

    first(turn[0])
    first(turn[1])
    for k in range(n_g + 1):
        if k < n_g:
            second(turn[k])
        if k + 2 < n_g:
            first(turn[k + 2])
        else:
            fill(share)
        if k >= 1:
            third(turn[k - 1])
    fill(depth // chunk)
    for s in range(1, n_g):
        take(0, 0, z_in.at[s - 1], z_sem.at[s - 1])
    result[...] = sums[0, 0]
    for k in range(max(depth // chunk - 2, 0), depth // chunk):
        out_copy(k).wait()
    for copy in started:
        copy.wait_send()


def reduce(b_turned, b_whole, hi, lo, n_g, n_u):
    depth, rows = b_turned.shape
    w = b_whole.shape[2]
    qs = depth // (2 * n_g)
    dma = pltpu.SemaphoreType.DMA
    chunk = next(k for k in (256, 128) if depth % k == 0)
    far = max(n_u - 1, 1)
    every = (n_g, 2 * n_u, qs, w)
    return pl.pallas_call(
        functools.partial(reduce_kernel, n_g, n_u, chunk),
        out_shape=(jax.ShapeDtypeStruct((rows, depth), F32), jax.ShapeDtypeStruct((qs, w), F32)),
        in_specs=[VMEM_SPEC, ANY_SPEC, VMEM_SPEC, VMEM_SPEC],
        out_specs=(ANY_SPEC, VMEM_SPEC),
        scratch_shapes=[
            pltpu.VMEM(b_whole.shape, b_whole.dtype),
            pltpu.VMEM((2, rows, chunk), F32),
            pltpu.VMEM(every, F32),
            pltpu.VMEM(every, BF16),
            pltpu.VMEM(every, BF16),
            pltpu.VMEM(every, BF16),
            pltpu.VMEM((n_g, far, qs, w), BF16),
            pltpu.VMEM((n_g, qs, w), BF16),
            pltpu.VMEM((n_g, far, qs, w), BF16),
            pltpu.VMEM((n_g, qs, w), BF16),
            dma,
            dma((2,)),
            dma(every[:2]),
            dma(every[:2]),
            dma(every[:2]),
            dma((n_g, far)),
            dma((n_g,)),
            dma((n_g, far)),
            dma((n_g,)),
        ],
        compiler_params=pltpu.CompilerParams(collective_id=2, has_side_effects=True, vmem_limit_bytes=LIMIT),
    )(b_turned, b_whole, hi, lo)


def on_device(n_occ, n_vir, b_occ, b_outer, eps_occ, eps_outer, eps_vir):
    n_g, n_u = n_occ // 2, n_vir // 2
    n_i, vl, depth = b_occ.shape
    n_j, _, qs = b_outer.shape
    own = b_outer.transpose(2, 0, 1).reshape(qs, n_j * vl)
    eps_rows = jnp.broadcast_to(eps_vir[None, :], (8, vl))
    flat = b_occ.reshape(n_i * vl, depth)
    b_whole, eps_all, b_turned = gather(own, eps_rows, flat, n_g, n_u)
    b_whole = b_whole.reshape(n_vir, depth, n_j * vl)
    hi, lo = amplitudes(flat, b_whole, eps_occ, eps_outer, eps_rows, eps_all)
    gamma_occ, mine = reduce(b_turned, b_whole, hi, lo, n_g, n_u)
    gamma_outer = mine.reshape(qs, n_j, vl).transpose(1, 2, 0)
    return gamma_occ.reshape(b_occ.shape), gamma_outer


def solution(mesh):
    placed = (P("occ", "vir", None), P(None, "vir", "occ"), P("occ"), P(), P("vir"))
    return jax.shard_map(
        functools.partial(on_device, mesh.shape["occ"], mesh.shape["vir"]),
        mesh=mesh,
        in_specs=placed,
        out_specs=(P("occ", "vir", None), P(None, "vir", "occ")),
        check_vma=False,
    )
```

```python
import functools

import jax
import jax.numpy as jnp
from jax import lax
from jax.experimental import pallas as pl
from jax.experimental.pallas import tpu as pltpu
from jax.sharding import PartitionSpec as P

MESH = pl.DeviceIdType.MESH
F32 = jnp.float32
BF16 = jnp.bfloat16
VMEM_SPEC = pl.BlockSpec(memory_space=pltpu.VMEM)
SMEM_SPEC = pl.BlockSpec(memory_space=pltpu.SMEM)
ANY_SPEC = pl.BlockSpec(memory_space=pl.ANY)
LIMIT = 62 * 1024 * 1024


def encode(x):
    square = x * x
    fourth = square * square
    return jnp.where(x < 0, -fourth, fourth).astype(BF16)


def decode(code):
    y = code.astype(F32)
    root = lax.rsqrt(lax.rsqrt(jnp.abs(y)))
    return jnp.where(y < 0, -root, root)


class Place:
    def __init__(self, n_g, n_u):
        o, v = lax.axis_index("occ"), lax.axis_index("vir")
        self.n_g, self.n_u = n_g, n_u
        self.o, self.v = o, v
        self.g, self.r = o // 2, o % 2
        self.u, self.c = v // 2, v % 2

    def up_g(self, s):
        return (self.g + s) % self.n_g

    def down_g(self, s):
        return (self.g + self.n_g - s) % self.n_g

    def up_u(self, t):
        return (self.u + t) % self.n_u

    def down_u(self, t):
        return (self.u + self.n_u - t) % self.n_u

    def x_peer(self):
        return (self.g * 2 + 1 - self.r, self.v)

    def c_peer(self):
        return (self.o, self.u * 2 + 1 - self.c)

    def y_peer(self, t):
        return (self.o, self.up_u(t) * 2 + self.c)

    def z_peer(self, s):
        return (self.up_g(s) * 2 + self.r, self.v)

    def greet(self, peers):
        barrier = pltpu.get_barrier_semaphore()
        for peer in peers:
            pl.semaphore_signal(barrier, inc=1, device_id=peer, device_id_type=MESH)
        pl.semaphore_wait(barrier, len(peers))


def remote(src, dst, send_sem, recv_sem, peer):
    return pltpu.make_async_remote_copy(
        src_ref=src, dst_ref=dst, send_sem=send_sem, recv_sem=recv_sem, device_id=peer, device_id_type=MESH
    )


def gather_kernel(n_g, n_u, own, eps, b_occ, out, eps_out, b_turned, b_in, b_out, local_sem, send, z_sem, x_sem, y_sem, d_sem, c_sem, e_send, e_sem):
    me = Place(n_g, n_u)
    n_vir = 2 * n_u
    fetch = pltpu.make_async_copy(b_occ, b_in, local_sem.at[2])
    fetch.start()
    vir_peers = [(me.o, (me.v + k) % n_vir) for k in range(1, n_vir)]
    me.greet([me.z_peer(s) for s in range(1, n_g)] + [me.x_peer()] + vir_peers)
    started = []

    def slot(g, r, u, c):
        return out.at[u * 2 + c, g * 2 + r]

    def go(src, place, recv_sem, peer):
        copy = remote(src, place, send.at[len(started)], recv_sem, peer)
        copy.start()
        started.append(copy)

    def arrived(place, sem):
        remote(place, place, send.at[0], sem, me.x_peer()).wait_recv()

    mine = slot(me.g, me.r, me.u, me.c)
    near = sorted(range(n_g), key=lambda s: (min(s, n_g - s), s))
    for s in near[1:]:
        go(own, mine, z_sem.at[s - 1], me.z_peer(s))
    go(own, mine, x_sem.at[0], me.x_peer())
    for t in range(1, n_u):
        go(own, mine, y_sem.at[0, t - 1], me.y_peer(t))
    go(own, mine, c_sem.at[0, 0, 0], me.c_peer())
    local = pltpu.make_async_copy(own, mine, local_sem.at[0])
    local.start()
    eps_local = pltpu.make_async_copy(eps, eps_out.at[me.v], local_sem.at[1])
    eps_local.start()
    eps_copies = [
        remote(eps, eps_out.at[me.v], e_send.at[k], e_sem.at[k], peer) for k, peer in enumerate(vir_peers)
    ]
    for copy in eps_copies:
        copy.start()

    def relay_z(s):
        place = slot(me.down_g(s), me.r, me.u, me.c)
        arrived(place, z_sem.at[s - 1])
        go(place, place, x_sem.at[s], me.x_peer())
        for t in range(1, n_u):
            go(place, place, y_sem.at[s, t - 1], me.y_peer(t))
        go(place, place, c_sem.at[s, 0, 0], me.c_peer())

    def relay_xy(s):
        place = slot(me.down_g(s), 1 - me.r, me.u, me.c)
        arrived(place, x_sem.at[s])
        if s % 2 == 0:
            for t in range(1, n_u):
                go(place, place, d_sem.at[s, t - 1], me.y_peer(t))
        go(place, place, c_sem.at[s, 1, 0], me.c_peer())
        for t in range(1, n_u):
            place = slot(me.down_g(s), me.r, me.down_u(t), me.c)
            arrived(place, y_sem.at[s, t - 1])
            if s % 2 == 1:
                go(place, place, d_sem.at[s, t - 1], me.x_peer())
            go(place, place, c_sem.at[s, 0, t], me.c_peer())

    depth = b_in.shape[1]
    tile = next(k for k in (256, 128) if depth % k == 0)

    def turn(k, carry):
        at = pl.ds(pl.multiple_of(k * tile, tile), tile)
        b_out[at, :] = b_in[:, at].T
        return carry

    tiles = depth // tile
    edges = [tiles * k // n_g for k in range(n_g + 1)]
    for k, s in enumerate(near):
        if k + 1 < n_g:
            relay_z(near[k + 1])
        if k == 0:
            fetch.wait()
        relay_xy(s)
        lax.fori_loop(edges[k], edges[k + 1], turn, 0)
    store = pltpu.make_async_copy(b_out, b_turned, local_sem.at[2])
    store.start()
    for s in near:
        for t in range(1, n_u):
            place = slot(me.down_g(s), 1 - me.r, me.down_u(t), me.c)
            arrived(place, d_sem.at[s, t - 1])
            go(place, place, c_sem.at[s, 1, t], me.c_peer())
    for s in range(n_g):
        for q in range(2):
            for t in range(n_u):
                r = me.r if q == 0 else 1 - me.r
                arrived(slot(me.down_g(s), r, me.down_u(t), 1 - me.c), c_sem.at[s, q, t])
    local.wait()
    eps_local.wait()
    store.wait()
    for k, copy in enumerate(eps_copies):
        copy.wait_send()
        source = (me.v + n_vir - 1 - k) % n_vir
        remote(eps, eps_out.at[source], e_send.at[k], e_sem.at[k], vir_peers[k]).wait_recv()
    for copy in started:
        copy.wait_send()


def gather(own, eps, b_occ, n_g, n_u):
    qs, w = own.shape
    n_vir = 2 * n_u
    dma = pltpu.SemaphoreType.DMA
    messages = (n_g - 1) + n_g + 2 * n_g * (n_u - 1) + 2 * n_g * n_u
    return pl.pallas_call(
        functools.partial(gather_kernel, n_g, n_u),
        out_shape=(
            jax.ShapeDtypeStruct((n_vir, 2 * n_g, qs, w), own.dtype),
            jax.ShapeDtypeStruct((n_vir,) + eps.shape, eps.dtype),
            jax.ShapeDtypeStruct(b_occ.shape[::-1], b_occ.dtype),
        ),
        in_specs=[VMEM_SPEC, VMEM_SPEC, ANY_SPEC],
        out_specs=(ANY_SPEC, VMEM_SPEC, ANY_SPEC),
        scratch_shapes=[
            pltpu.VMEM(b_occ.shape, b_occ.dtype),
            pltpu.VMEM(b_occ.shape[::-1], b_occ.dtype),
            dma((3,)),
            dma((messages,)),
            dma((n_g,)),
            dma((n_g,)),
            dma((n_g, max(n_u - 1, 1))),
            dma((n_g, max(n_u - 1, 1))),
            dma((n_g, 2, n_u)),
            dma((n_vir - 1,)),
            dma((n_vir - 1,)),
        ],
        compiler_params=pltpu.CompilerParams(collective_id=0, has_side_effects=True, vmem_limit_bytes=LIMIT),
    )(own, eps, b_occ)


def window_kernel(
    n_g, n_u, n_i, n_j, chunk, b_occ, b_turned_all, b_whole, e_occ, e_outer, e_mine, e_all, gamma, result,
    hi, lo, amps, sent, got, b_turned,
    b_local, held, sums, c_out, c_in, out, d_in, x_in, y_in, z_in,
    f_sem, send_sem, recv_sem, b_sem, g_sem, c_send, c_sem, send, d_sem, x_sem, y_sem, z_sem,
):
    o, v = lax.axis_index("occ"), lax.axis_index("vir")
    u, c, n_vir = v // 2, v % 2, 2 * n_u
    steps = [(t, e) for t in range(1, n_u) for e in range(2)] + [(0, 1), (0, 0)]
    far = n_vir - 1
    targets = [(u + t) % n_u * 2 + (c + e) % 2 for t, e in steps]
    sources = [(u + n_u - t) % n_u * 2 + (c + e) % 2 for t, e in steps]
    rows = b_occ.shape[0]
    vl = rows // n_i

    def load(k):
        return pltpu.make_async_copy(b_whole.at[targets[k]], b_local.at[targets[k]], b_sem.at[k])

    for k in range(n_vir):
        load(k).start()
    fetch = pltpu.make_async_copy(b_turned_all, b_turned, f_sem)
    fetch.start()
    me = Place(n_g, n_u)
    me.greet(
        [(o, peer) for peer in targets[:far]] + [me.z_peer(s) for s in range(1, n_g)] + [me.x_peer()]
    )

    row = e_mine[...].T[:, 0:1]
    copies = []
    for k, target in enumerate(targets):
        load(k).wait()
        amps[target] = jnp.dot(b_occ[...], b_local[target], preferred_element_type=F32)
        col = jnp.concatenate([e_outer[j] - e_all[target, 0:1, :] for j in range(n_j)], axis=1)

        def divide(i, carry, k=k, target=target, col=col):
            at = pl.ds(pl.multiple_of(i * vl, vl), vl)
            value = amps[target, at, :] / ((e_occ[i] - row) + col)
            amps[target, at, :] = value
            code = encode(value)
            if k < far:
                sent[k, at, :] = code
            else:
                got[target, at, :] = code
            return carry

        lax.fori_loop(0, n_i, divide, 0)
        if k < far:
            copy = remote(sent.at[k], got.at[v], send_sem.at[k], recv_sem.at[k], (o, target))
            copy.start()
            copies.append(copy)

    def finish(source):
        def part(i, carry):
            at = pl.ds(pl.multiple_of(i * vl, vl), vl)
            turned = decode(got[source, at, :]).T
            swapped = jnp.concatenate([turned[j * vl : (j + 1) * vl] for j in range(n_j)], axis=1)
            tilde = 2.0 * amps[source, at, :] - swapped
            high = tilde.astype(BF16)
            hi[source, at, :] = high
            lo[source, at, :] = (tilde - high.astype(F32)).astype(BF16)
            return carry

        lax.fori_loop(0, n_i, part, 0)

    def collect(k):
        source = sources[k]
        remote(sent.at[k], got.at[source], send_sem.at[k], recv_sem.at[k], (o, source)).wait_recv()
        finish(source)

    finish(v)
    collect(far - 1)
    fetch.wait()
    qs = c_out.shape[2]
    depth = b_whole.shape[1]
    started = []

    def product(s, t, c, store):
        g = (me.g + s) % n_g
        v = (me.u + t) % n_u * 2 + c
        at = pl.ds(pl.multiple_of(g * 2 * qs, 2 * qs), 2 * qs)
        both = jnp.dot(
            b_turned[at, :], jnp.concatenate([hi[v], lo[v]], axis=1), preferred_element_type=F32
        )
        width = hi.shape[2]
        both = both[:, :width] + both[:, width:]
        store(me.r * n_u + t, both[:qs])
        store((1 - me.r) * n_u + t, both[qs:])

    def go(src, dst, send_sem, recv_sem, peer):
        copy = remote(src, dst, send_sem, recv_sem, peer)
        copy.start()
        started.append(copy)

    def arrived(dst, sem):
        remote(dst, dst, sem, sem, me.x_peer()).wait_recv()

    def ship(s, q, dst, sem, peer):
        out[s, q] = encode(sums[s, q])
        go(out.at[s, q], dst, send.at[s, q], sem, peer)

    def take(s, q, src, sem):
        arrived(src, sem)
        sums[s, q] = sums[s, q] + decode(src[...])

    done = [0]

    def out_copy(k):
        slot = k % 2
        at = pl.ds(pl.multiple_of(k * chunk, chunk), chunk)
        return pltpu.make_async_copy(held.at[slot], gamma.at[:, at], g_sem.at[slot])

    def fill(count):
        def part(k, carry):
            @pl.when(k >= 2)
            def _():
                out_copy(k - 2).wait()

            at = pl.ds(pl.multiple_of(k * chunk, chunk), chunk)
            right = jnp.concatenate([b_local[v, at, :] for v in range(n_vir)], axis=1)
            total = None
            for part_of in (hi, lo):
                left = jnp.concatenate([part_of[v] for v in range(n_vir)], axis=1)
                term = lax.dot_general(left, right, (((1,), (1,)), ((), ())), preferred_element_type=F32)
                total = term if total is None else total + term
            held[k % 2] = total
            out_copy(k).start()
            return carry

        last = min(done[0] + count, depth // chunk)
        if last > done[0]:
            lax.fori_loop(done[0], last, part, 0)
        done[0] = last

    share = max(depth // chunk // 4, 1)
    turn = [s % n_g for s in range(1, n_g + 1)]

    def multiply(s, first_t, last_t):
        def keep(q, value):
            sums[s, q] = value

        def code(q, value):
            c_out[s, q] = encode(value)

        def theirs(t, carry):
            product(s, t, 1 - me.c, code)
            return carry

        def ours(t, carry):
            product(s, t, me.c, keep)
            return carry

        lax.fori_loop(first_t, last_t, theirs, 0)
        for t in range(first_t, last_t):
            for q in (t, n_u + t):
                go(c_out.at[s, q], c_in.at[s, q], c_send.at[s, q], c_sem.at[s, q], me.c_peer())
        lax.fori_loop(first_t, last_t, ours, 0)

    def first(s):
        multiply(s, 1, n_u)
        for q in reversed(range(2 * n_u)):
            take(s, q, c_in.at[s, q], c_sem.at[s, q])
            t = q - n_u
            if t > 0:
                peer = me.y_peer(t) if s % 2 == 0 else me.x_peer()
                ship(s, q, d_in.at[s, t - 1], d_sem.at[s, t - 1], peer)
        if s % 2 == 0:
            for t in range(1, n_u):
                ship(s, t, y_in.at[s, t - 1], y_sem.at[s, t - 1], me.y_peer(t))
        else:
            ship(s, n_u, x_in.at[s], x_sem.at[s], me.x_peer())

    def second(s):
        for t in range(1, n_u):
            q = n_u if s % 2 == 0 else t
            take(s, q, d_in.at[s, t - 1], d_sem.at[s, t - 1])
        if s % 2 == 0:
            ship(s, n_u, x_in.at[s], x_sem.at[s], me.x_peer())
        else:
            for t in range(1, n_u):
                ship(s, t, y_in.at[s, t - 1], y_sem.at[s, t - 1], me.y_peer(t))

    def third(s):
        take(s, 0, x_in.at[s], x_sem.at[s])
        for t in range(1, n_u):
            take(s, 0, y_in.at[s, t - 1], y_sem.at[s, t - 1])
        if s:
            ship(s, 0, z_in.at[s - 1], z_sem.at[s - 1], me.z_peer(s))

    for s in turn:
        multiply(s, 0, 1)
    for k in range(far - 1):
        collect(k)
    first(turn[0])
    first(turn[1])
    for k in range(n_g + 1):
        if k < n_g:
            second(turn[k])
        if k + 2 < n_g:
            first(turn[k + 2])
        else:
            fill(share)
        if k >= 1:
            third(turn[k - 1])
    fill(depth // chunk)
    for s in range(1, n_g):
        take(0, 0, z_in.at[s - 1], z_sem.at[s - 1])
    result[...] = sums[0, 0]
    for k in range(max(depth // chunk - 2, 0), depth // chunk):
        out_copy(k).wait()
    for copy in started + copies:
        copy.wait_send()


def window(b_occ, b_turned, b_whole, e_occ, e_outer, e_mine, e_all, n_g, n_u):
    n_vir, n_i, n_j = 2 * n_u, e_occ.shape[0], e_outer.shape[0]
    depth, rows = b_turned.shape
    w = b_whole.shape[2]
    qs = depth // (2 * n_g)
    dma = pltpu.SemaphoreType.DMA
    chunk = next(k for k in (256, 128) if depth % k == 0)
    far = max(n_u - 1, 1)
    every = (n_g, 2 * n_u, qs, w)
    return pl.pallas_call(
        functools.partial(window_kernel, n_g, n_u, n_i, n_j, chunk),
        out_shape=(jax.ShapeDtypeStruct((rows, depth), F32), jax.ShapeDtypeStruct((qs, w), F32)),
        in_specs=[VMEM_SPEC, ANY_SPEC, ANY_SPEC, SMEM_SPEC, SMEM_SPEC, VMEM_SPEC, VMEM_SPEC],
        out_specs=(ANY_SPEC, VMEM_SPEC),
        scratch_shapes=[
            pltpu.VMEM((n_vir, rows, w), BF16),
            pltpu.VMEM((n_vir, rows, w), BF16),
            pltpu.VMEM((n_vir, rows, w), F32),
            pltpu.VMEM((n_vir - 1, rows, w), BF16),
            pltpu.VMEM((n_vir, rows, w), BF16),
            pltpu.VMEM(b_turned.shape, BF16),
            pltpu.VMEM(b_whole.shape, b_whole.dtype),
            pltpu.VMEM((2, rows, chunk), F32),
            pltpu.VMEM(every, F32),
            pltpu.VMEM(every, BF16),
            pltpu.VMEM(every, BF16),
            pltpu.VMEM(every, BF16),
            pltpu.VMEM((n_g, far, qs, w), BF16),
            pltpu.VMEM((n_g, qs, w), BF16),
            pltpu.VMEM((n_g, far, qs, w), BF16),
            pltpu.VMEM((n_g, qs, w), BF16),
            dma,
            dma((n_vir - 1,)),
            dma((n_vir - 1,)),
            dma((n_vir,)),
            dma((2,)),
            dma(every[:2]),
            dma(every[:2]),
            dma(every[:2]),
            dma((n_g, far)),
            dma((n_g,)),
            dma((n_g, far)),
            dma((n_g,)),
        ],
        compiler_params=pltpu.CompilerParams(collective_id=1, has_side_effects=True, vmem_limit_bytes=LIMIT),
    )(b_occ, b_turned, b_whole, e_occ, e_outer, e_mine, e_all)


def on_device(n_occ, n_vir, b_occ, b_outer, eps_occ, eps_outer, eps_vir):
    n_g, n_u = n_occ // 2, n_vir // 2
    n_i, vl, depth = b_occ.shape
    n_j, _, qs = b_outer.shape
    own = b_outer.transpose(2, 0, 1).reshape(qs, n_j * vl)
    eps_rows = jnp.broadcast_to(eps_vir[None, :], (8, vl))
    flat = b_occ.reshape(n_i * vl, depth)
    b_whole, eps_all, b_turned = gather(own, eps_rows, flat, n_g, n_u)
    b_whole = b_whole.reshape(n_vir, depth, n_j * vl)
    gamma_occ, mine = window(flat, b_turned, b_whole, eps_occ, eps_outer, eps_rows, eps_all, n_g, n_u)
    gamma_outer = mine.reshape(qs, n_j, vl).transpose(1, 2, 0)
    return gamma_occ.reshape(b_occ.shape), gamma_outer


def solution(mesh):
    placed = (P("occ", "vir", None), P(None, "vir", "occ"), P("occ"), P(), P("vir"))
    return jax.shard_map(
        functools.partial(on_device, mesh.shape["occ"], mesh.shape["vir"]),
        mesh=mesh,
        in_specs=placed,
        out_specs=(P("occ", "vir", None), P(None, "vir", "occ")),
        check_vma=False,
    )
```
